32 devices in a mesh: expert: 4 (over z), dp: 4 (over y, core), replica: 2 (over x).
Axes of the slice: x: 2, y: 2, z: 4, core: 2. Of those that a mesh axis runs over, the one named last changes fastest.
Arguments:
- cotangent: bfloat16 [2, 4, 4, 128, 2048], P('replica', 'expert', 'dp'), may hold values from -0.5 to 0.5
- expert_ids: int32 [2, 4, 4, 128, 2], P('replica', 'expert', 'dp'), may hold values from 0 to 3, all different within a row; in each aligned block of 128 rows (0 to 127, 128 to 255, ..., all dimensions but the last counted through in order) at most 96 rows name the same one
- gate_values: float32 [2, 4, 4, 128, 2], P('replica', 'expert', 'dp'), may hold values from 0.1 to 1
- hidden_saved: bfloat16 [2, 4, 4, 4, 4, 24, 7168], P('replica', 'expert', 'dp'), may hold values from -6 to 6
- output_saved: bfloat16 [2, 4, 4, 4, 4, 24, 2048], P('replica', 'expert', 'dp'), may hold values from -6 to 6
- weights: bfloat16 [2, 4, 7168, 2048], P('replica', 'expert', 'dp'), may hold values from -6 to 6
- moment_one: bfloat16 [2, 4, 7168, 2048], P('replica', 'expert', 'dp'), may hold values from -4 to 4
- moment_two: bfloat16 [2, 4, 7168, 2048], P('replica', 'expert', 'dp'), may hold values from 0.19921875 to 2
- anchor: float32 [4, 1792, 2048], P('expert', 'dp'), may hold values from -6 to 6
- outer_moment: float32 [4, 1792, 2048], P('expert', 'dp'), may hold values from -2 to 2
Outputs:
- new_weights: bfloat16 [2, 4, 7168, 2048], P('replica', 'expert', 'dp')
- gate_grads: float32 [2, 4, 4, 128, 2], P('replica', 'expert', 'dp')
- grad_rms: float32 [2], P('replica')
The draws below stay inside these ranges and needn't reach their ends.
Inputs may be any that keep to these rules, and one draw needn't show every extreme that they name: `expert_ids`: each token names two different experts; among the 128 tokens of one device no expert is named more than 96 times, a bound that some block reaches.
All inputs are finite; a program needn't handle non-finite values.
Results may differ from the reference program's by a relative error of at most 0.0075.
Values may be sent and summed in bfloat16 or wider, within the bound.
A program may use at most 192 MiB of HBM per device.

```python
import math
import jax
import jax.numpy as jnp
import numpy as np
from jax import lax

D = 2048
FF = 7168
TOK_DEV = 128
EXPERTS = 4
MOST = 96
CAP = 24
FRAG = 1792
N_EXPERT = 4
N_DP = 4
N_REPLICA = 2


def block_levels(stream_key, dims, split, least, top_value):
    gain = 1.0
    for axis_at, shards_of in split:
        steps = jax.random.uniform(jax.random.fold_in(jax.random.fold_in(stream_key, 6), axis_at), (shards_of,), jnp.float32, least / len(split), top_value / len(split))
        gain = gain * jnp.repeat(jnp.exp(steps), dims[axis_at] // shards_of).reshape((-1,) + (1,) * (len(dims) - 1 - axis_at))
    return gain


def routed_block(rng, own, number, rows, amount, top, most, lean):
    sequence = jax.random.permutation(rng, amount)
    crowded, common = portions_of(amount, rows * top, most, lean, True), portions_of(amount, rows * top, most, lean, False)
    places = jnp.arange(amount)

    def named(tallies, rotation):
        used = int((tallies > 0).sum())
        fixed = max(1, used // 4)
        passed = fixed + (places - fixed + rotation * (used - fixed)) % max(1, amount - fixed)
        return jnp.zeros((amount,), jnp.int32).at[sequence[jnp.where(places < fixed, places, passed)]].set(jnp.asarray(tallies, jnp.int32))

    tallies = jnp.where(number % 4 == 0, named(crowded, number // 4), named(common, number - number // 4 - 1))
    mixed = jax.random.permutation(jax.random.fold_in(own, 3), amount)
    donor, sink = mixed[0:amount // 2 * 2:2], mixed[1:amount // 2 * 2:2]
    slack = jnp.minimum(tallies[donor] - 1, most - tallies[sink]) // 2
    slack = jnp.where((donor == sequence[0]) | (sink == sequence[0]) | (tallies[sink] == 0), 0, jnp.maximum(slack, 0))
    passed = jax.random.randint(jax.random.fold_in(own, 4), (amount // 2,), 0, 1 << 20) % (slack + 1)
    tallies = tallies.at[donor].add(-passed).at[sink].add(passed)
    items = jnp.searchsorted(jnp.cumsum(tallies), jnp.arange(rows * top), side="right").astype(jnp.int32)
    table = items.reshape(top, rows).T
    table = table[jax.random.permutation(jax.random.fold_in(own, 1), rows)]
    rotation = jax.random.randint(jax.random.fold_in(own, 2), (rows, 1), 0, top)
    return jnp.take_along_axis(table, (jnp.arange(top)[None, :] + rotation) % top, axis=1)


def portions_of(count, total, most, lean, full):
    weights = [(1 << 20) // math.isqrt(standing ** lean) + 1 for standing in range(1, count + 1)]
    largest = most if full else min(most, max(-(-total // count), total * weights[0] // sum(weights)))
    least = 1 if total - largest >= count - 1 else 0
    holding, surplus = [largest] + [least] * (count - 1), total - largest - least * (count - 1)
    while surplus > 0:
        free = [i for i in range(1, count) if holding[i] < largest] or [i for i in range(1, count) if holding[i] < most]
        mass, remaining = sum([weights[i] for i in free]), surplus
        for i in free:
            addition = min(most - holding[i], max(1, remaining * weights[i] // mass), surplus)
            holding[i] = holding[i] + addition
            surplus = surplus - addition
    return np.array(holding)


def normal_values(stream_key, extent, spread, most, cuts=(), kind=jnp.bfloat16):
    drawn = spread * jax.random.normal(stream_key, extent, jnp.float32)
    if cuts:
        drawn = drawn * block_levels(stream_key, extent, cuts, -0.22, 0.18)
    return jnp.clip(drawn, -most, most).astype(kind)


def setup_inputs(seed: int = 0) -> dict:
    splits = jax.random.split(jax.random.key(seed), 11)
    cotangent = normal_values(splits[0], (N_REPLICA, N_EXPERT, N_DP, TOK_DEV, D), 0.0625, 0.5, ((0, 2), (1, 4), (2, 4)))
    expert_ids_keys = jax.random.split(jax.random.fold_in(splits[1], 1), N_REPLICA * N_EXPERT * N_DP * TOK_DEV // TOK_DEV)
    expert_ids_turns = jax.random.permutation(jax.random.fold_in(splits[1], 3), N_REPLICA * N_EXPERT * N_DP * TOK_DEV // TOK_DEV)
    expert_ids = jax.vmap(lambda own, number: routed_block(jax.random.fold_in(splits[1], 2), own, number, TOK_DEV, EXPERTS, 2, MOST, 2))(expert_ids_keys, expert_ids_turns).reshape((N_REPLICA, N_EXPERT, N_DP, TOK_DEV, 2))
    gate_values = jnp.clip(0.1 + 0.9 * jax.random.uniform(splits[2], (N_REPLICA, N_EXPERT, N_DP, TOK_DEV, 2), jnp.float32) ** block_levels(splits[2], (N_REPLICA, N_EXPERT, N_DP, TOK_DEV, 2), ((0, 2), (1, 4), (2, 4)), -0.2, 0.2), 0.1, 1.0)
    hidden_saved = normal_values(splits[3], (N_REPLICA, EXPERTS, N_DP, N_EXPERT, N_DP, CAP, FF), 1.0, 6.0, ((0, 2), (1, 4), (2, 4)))
    output_saved = normal_values(splits[4], (N_REPLICA, EXPERTS, N_DP, N_EXPERT, N_DP, CAP, D), 1.0, 6.0, ((0, 2), (1, 4), (2, 4)))
    weights = normal_values(splits[5], (N_REPLICA, EXPERTS, FF, D), 1.0, 6.0, ((0, 2), (1, 4), (2, 4)))
    moment_one = normal_values(splits[6], (N_REPLICA, EXPERTS, FF, D), 0.5, 4.0, ((0, 2), (1, 4), (2, 4)))
    moment_two = jnp.clip(jnp.exp(math.log(2.0) - 2.306499 * jax.random.uniform(splits[7], (N_REPLICA, EXPERTS, FF, D), jnp.float32) ** block_levels(splits[7], (N_REPLICA, EXPERTS, FF, D), ((0, 2), (1, 4), (2, 4)), -0.2, 0.2)), 0.19921875, 2.0).astype(jnp.bfloat16)
    anchor = normal_values(splits[8], (EXPERTS, FRAG, D), 1.0, 6.0, ((0, 4), (1, 4)), jnp.float32)
    outer_moment = normal_values(splits[9], (EXPERTS, FRAG, D), 0.3, 2.0, ((0, 4), (1, 4)), jnp.float32)
    return dict(cotangent=cotangent, expert_ids=expert_ids, gate_values=gate_values, hidden_saved=hidden_saved, output_saved=output_saved, weights=weights, moment_one=moment_one, moment_two=moment_two, anchor=anchor, outer_moment=outer_moment)


beta_one = 0.9
beta_two = 0.95
epsilon = 1e-08
inner_rate = 0.3
weight_decay = 0.1
outer_rate = 0.7
nesterov_coef = 0.9

def slot_places(expert_ids):
    chosen = expert_ids.reshape(expert_ids.shape[:-2] + (-1,))
    onehot = (chosen[..., None] == jnp.arange(EXPERTS, dtype=jnp.int32)).astype(jnp.int32)
    before = jnp.cumsum(onehot, axis=-2) - onehot
    order_rank = lax.optimization_barrier(jnp.sum(before * onehot, axis=-1))
    return (chosen, order_rank % N_DP, order_rank // N_DP)

def expert_update(packed):
    hidden_e, slots_e, weight_e, first_e, second_e = packed

    def add_holder(summed, pair):
        hidden_rows, slot_rows = pair
        partial_term = jnp.dot(hidden_rows.reshape(-1, FF).astype(jnp.float32).T, slot_rows.reshape(-1, D).astype(jnp.float32), preferred_element_type=jnp.float32)
        partial_term = lax.optimization_barrier(partial_term.astype(jnp.bfloat16)).astype(jnp.float32)
        return (summed + partial_term, None)
    gradient, _ = lax.scan(add_holder, jnp.zeros((FF, D), jnp.float32), (hidden_e, slots_e))
    squares = jnp.sum(gradient * gradient)
    first_new = beta_one * first_e.astype(jnp.float32) + (1.0 - beta_one) * gradient
    second_new = beta_two * second_e.astype(jnp.float32) + (1.0 - beta_two) * gradient * gradient
    weight_old = weight_e.astype(jnp.float32)
    inner_new = weight_old - inner_rate * (first_new / (jnp.sqrt(second_new) + epsilon) + weight_decay * weight_old)
    return (inner_new.astype(jnp.bfloat16), squares)

def reference(cotangent, expert_ids, gate_values, hidden_saved, output_saved, weights, moment_one, moment_two, anchor, outer_moment):
    chosen, holder, slot_index = slot_places(expert_ids)
    replica_idx = jnp.arange(N_REPLICA, dtype=jnp.int32)[:, None, None, None]
    source_exp = jnp.arange(N_EXPERT, dtype=jnp.int32)[None, :, None, None]
    source_dp = jnp.arange(N_DP, dtype=jnp.int32)[None, None, :, None]
    picked = output_saved[replica_idx, chosen, holder, source_exp, source_dp, slot_index]
    picked = picked.reshape(N_REPLICA, N_EXPERT, N_DP, TOK_DEV, 2, D)
    upstream = cotangent.astype(jnp.float32)
    gate_grads = jnp.einsum('abctkd,abctd->abctk', picked.astype(jnp.float32), upstream)
    sends = (gate_values[..., None] * upstream[..., None, :]).astype(jnp.bfloat16)
    sends = sends.reshape(N_REPLICA, N_EXPERT, N_DP, 2 * TOK_DEV, D)
    slot_values = jnp.zeros(output_saved.shape, jnp.bfloat16)
    slot_values = slot_values.at[replica_idx, chosen, holder, source_exp, source_dp, slot_index].set(sends)
    inner_list = []
    rms_list = []
    for replica in range(N_REPLICA):
        inner_new, squares = lax.map(expert_update, (hidden_saved[replica], slot_values[replica], weights[replica], moment_one[replica], moment_two[replica]))
        inner_list.append(inner_new)
        rms_list.append(jnp.sqrt(jnp.sum(squares) / (EXPERTS * FF * D)))
    summed = jnp.zeros(anchor.shape, jnp.float32)
    for replica in range(N_REPLICA):
        summed = summed + (anchor - inner_list[replica][:, 0::4, :].astype(jnp.float32))
    average = summed / N_REPLICA
    momentum = nesterov_coef * outer_moment + average
    new_anchor = (anchor - outer_rate * (average + nesterov_coef * momentum)).astype(jnp.bfloat16)
    new_weights = jnp.stack([inner_list[replica].at[:, 0::4, :].set(new_anchor) for replica in range(N_REPLICA)])
    grad_rms = jnp.stack(rms_list).astype(jnp.float32)
    return (new_weights, gate_grads, grad_rms)
```

```python
import functools

import jax
import jax.numpy as jnp
from jax import lax
from jax.experimental import pallas as pl
from jax.experimental.pallas import tpu as pltpu
from jax.sharding import PartitionSpec as P

beta_one = 0.9
beta_two = 0.95
epsilon = 1e-08
inner_rate = 0.3
weight_decay = 0.1
outer_rate = 0.7
nesterov_coef = 0.9

MESH = pl.DeviceIdType.MESH
BF = jnp.bfloat16
F32 = jnp.float32


def kernel(
    dims,
    ids_ref, gates_ref, cot_ref, hid_ref, osv_ref, w_ref, m1_ref, m2_ref, anc_ref, om_ref,
    out_ref, gg_ref, rms_ref,
    hid, hidt, slots, sends, wbuf, m1buf, m2buf, ancbuf, ombuf, osv, cot,
    frag_send, frag_recv, tmp, gg_acc, sq_acc, msg_send, msg_recv,
    load_sem, out_sem, hs_sem, hr_sem, zs_sem, zr_sem, ys_sem, yr_sem, ps_sem, pr_sem,
    xs_sem, xr_sem, ms_sem, mr_sem,
):
    n_exp, n_dp, n_rep, cap, rows, width, full, nj, rblk = dims
    dc = width // nj
    n_src = n_exp * n_dp
    per = n_src * cap
    depth = n_dp * per
    n_y = n_dp // 2
    e = lax.axis_index("expert")
    d = lax.axis_index("dp")
    r = lax.axis_index("replica")
    me = e * n_dp + d
    core = lax.rem(d, 2)
    yy = d // 2
    partner = yy * 2 + 1 - core
    other = lax.rem(r + 1, n_rep)

    def cols(j):
        return pl.ds(j * dc, dc)

    def remote(src, dst, ssem, rsem, to):
        return pltpu.make_async_remote_copy(
            src_ref=src, dst_ref=dst, send_sem=ssem, recv_sem=rsem,
            device_id=to, device_id_type=MESH,
        )

    def mod(x, n):
        return lax.rem(x + 2 * n, n)

    loads = []
    for i, (src, dst) in enumerate([
        (cot_ref, cot), (osv_ref, osv), (w_ref, wbuf), (m1_ref, m1buf),
        (m2_ref, m2buf), (anc_ref, ancbuf), (om_ref, ombuf),
    ]):
        loads.append(pltpu.make_async_copy(src, dst, load_sem.at[i]))
    loads[0].start()

    def hid_cols(to):
        return pl.ds(pl.multiple_of(to * rows, 128), rows)

    hid_own = pltpu.make_async_copy(hid_ref.at[:, :, :, hid_cols(d)], hid.at[d], load_sem.at[7])

    barrier = pltpu.get_barrier_semaphore()
    for k in range(1, n_src):
        to = mod(me + k, n_src)
        pl.semaphore_signal(barrier, inc=1, device_id={"expert": to // n_dp, "dp": lax.rem(to, n_dp)}, device_id_type=MESH)
    pl.semaphore_signal(barrier, inc=1, device_id={"replica": other}, device_id_type=MESH)
    pl.semaphore_wait(barrier, n_src)

    hid_sends = []
    for k in range(2, n_dp + 1):
        to = mod(d + k, n_dp) if k < n_dp else partner
        if k < n_dp:
            q = (k - 2) // 2 + 1
            yto = mod(yy + q, n_y)
            to = yto * 2 + lax.rem(k, 2)
        hid_sends.append(remote(
            hid_ref.at[:, :, :, hid_cols(to)], hid.at[d],
            hs_sem.at[k - 2], hr_sem.at[d], {"dp": to},
        ))
        hid_sends[-1].start()
    hid_own.start()
    for c in loads[1:]:
        c.start()

    ids0, ids1 = ids_ref[0:1, :], ids_ref[1:2, :]
    toks = ids_ref.shape[1]
    erow = lax.broadcasted_iota(jnp.int32, (8 * ((n_exp + 7) // 8), toks), 0)
    counts = ((ids0 == erow).astype(F32) + (ids1 == erow).astype(F32)).astype(BF)
    earlier = (
        lax.broadcasted_iota(jnp.int32, (toks, toks), 0) < lax.broadcasted_iota(jnp.int32, (toks, toks), 1)
    ).astype(F32).astype(BF)
    ranks = jnp.dot(counts, earlier, preferred_element_type=F32)
    shift = n_dp.bit_length() - 1

    def place(ids):
        rank = jnp.sum(jnp.where(ids == erow, ranks, 0.0), axis=0, keepdims=True).astype(jnp.int32)
        return (ids * n_dp + (rank & (n_dp - 1))) * cap + (rank >> shift)

    place0, place1 = place(ids0), place(ids1)
    gate0, gate1 = gates_ref[0:1, :], gates_ref[1:2, :]
    srow = lax.broadcasted_iota(jnp.int32, (per, toks), 0)
    gate_slot = jnp.sum(
        jnp.where(srow == place0, gate0, 0.0) + jnp.where(srow == place1, gate1, 0.0), axis=1, keepdims=True
    )
    onehot = ((srow == place0).astype(F32) + (srow == place1).astype(F32)).astype(BF)
    loads[0].wait()
    z_sends = []
    for j in range(nj):
        rows_j = jnp.dot(onehot, cot[:, j * dc:(j + 1) * dc], preferred_element_type=F32)
        sends[:, :, :, j * dc:(j + 1) * dc] = (gate_slot * rows_j).astype(BF).reshape(n_exp, n_dp, cap, dc)
        for k in range(1, n_exp):
            to = mod(e + k, n_exp)
            z_sends.append(remote(
                sends.at[to, :, :, cols(j)], slots.at[:, e, d, :, cols(j)],
                zs_sem.at[k - 1, j], zr_sem.at[e, j], {"expert": to},
            ))
            z_sends[-1].start()
        slots[:, pl.ds(e, 1), pl.ds(d, 1), :, j * dc:(j + 1) * dc] = (
            sends[pl.ds(e, 1), :, :, j * dc:(j + 1) * dc].reshape(n_dp, 1, 1, cap, dc)
        )

    fwd = []
    for j in range(nj):
        for k in range(1, n_exp):
            a = mod(e + k, n_exp)
            remote(
                sends.at[a, :, :, cols(j)], slots.at[:, a, d, :, cols(j)],
                zs_sem.at[k - 1, j], zr_sem.at[a, j], {"expert": a},
            ).wait_recv()
        mine = slots.at[:, :, d, :, cols(j)]
        for q in range(1, n_y):
            to = mod(yy + q, n_y) * 2 + core
            fwd.append(remote(mine, mine, ys_sem.at[q - 1, j], yr_sem.at[yy, j], {"dp": to}))
            fwd[-1].start()
        fwd.append(remote(mine, mine, ps_sem.at[0, j], pr_sem.at[yy, j], {"dp": partner}))
        fwd[-1].start()

    def turn(h):
        for s in range(0, rows, 128):
            block = hid[pl.ds(h, 1), :, :, :, s:s + 128].reshape(per, 128)
            hidt[s:s + 128, pl.ds(pl.multiple_of(h * per, 128), per)] = block.T

    hid_own.wait()
    turn(d)
    for k in range(n_dp, 1, -1):
        if k < n_dp:
            q = (k - 2) // 2 + 1
            h = mod(yy - q, n_y) * 2 + lax.rem(k, 2)
        else:
            h = partner
        remote(hid.at[h], hid.at[h], hs_sem.at[k - 2], hr_sem.at[h], {"dp": h}).wait_recv()
        turn(h)
    for c in loads[1:]:
        c.wait()

    sq_acc[...] = jnp.zeros_like(sq_acc)
    gg_acc[...] = jnp.zeros_like(gg_acc)
    x_sends, outs = [], []
    fblk = rblk // 4

    def main(j):
        lo, hi = j * dc, (j + 1) * dc
        right = slots[:, :, :, :, lo:hi].reshape(depth, dc)
        prod = (
            slots[pl.ds(d, 1), :, :, :, lo:hi].reshape(per, dc).astype(F32)
            * osv[:, :, :, lo:hi].reshape(per, dc).astype(F32)
        )
        part = prod[:, :128]
        for s in range(128, dc, 128):
            part = part + prod[:, s:s + 128]
        gg_acc[...] += part

        def step(i, _):
            here = pl.ds(pl.multiple_of(i * rblk, rblk), rblk)
            g = jnp.dot(hidt[here, :], right, preferred_element_type=F32)
            sq_acc[...] += jnp.sum((g * g).reshape(rblk // 8, 8, dc), axis=0)
            first = beta_one * m1buf[here, lo:hi].astype(F32) + (1.0 - beta_one) * g
            second = beta_two * m2buf[here, lo:hi].astype(F32) + (1.0 - beta_two) * g * g
            old = wbuf[here, lo:hi].astype(F32)
            new = old - inner_rate * (first / (jnp.sqrt(second) + epsilon) + weight_decay * old)
            wbuf[here, lo:hi] = new.astype(BF)
            for s in range(0, dc, 128):
                tmp[s // 128] = new[:, s:s + 128]
                frag_send[pl.ds(pl.multiple_of(i * fblk, fblk), fblk), lo + s:lo + s + 128] = (
                    tmp[s // 128, pl.ds(0, fblk, stride=4), :].astype(BF)
                )
            return 0

        lax.fori_loop(0, rows // rblk, step, 0)
        x_sends.append(remote(
            frag_send.at[:, cols(j)], frag_recv.at[:, cols(j)], xs_sem.at[j], xr_sem.at[j], {"replica": other}
        ))
        x_sends[-1].start()

    def merge(j):
        lo, hi = j * dc, (j + 1) * dc
        x_sends[j].wait_recv()

        def step(i, _):
            here = pl.ds(pl.multiple_of(i * rblk, rblk), rblk)
            there = pl.ds(pl.multiple_of(i * fblk, fblk), fblk)
            start = ancbuf[there, lo:hi]
            summed = (start - frag_send[there, lo:hi].astype(F32)) + (start - frag_recv[there, lo:hi].astype(F32))
            average = summed / n_rep
            momentum = nesterov_coef * ombuf[there, lo:hi] + average
            point = start - outer_rate * (average + nesterov_coef * momentum)
            for s in range(0, dc, 128):
                tmp[s // 128] = wbuf[here, lo + s:lo + s + 128].astype(F32)
                tmp[s // 128, pl.ds(0, fblk, stride=4), :] = point[:, s:s + 128]
                wbuf[here, lo + s:lo + s + 128] = tmp[s // 128].astype(BF)
            return 0

        lax.fori_loop(0, rows // rblk, step, 0)
        outs.append(pltpu.make_async_copy(wbuf.at[:, cols(j)], out_ref.at[:, cols(j)], out_sem.at[j]))
        outs[-1].start()

    for j in range(nj):
        for q in range(1, n_y):
            yfrom = mod(yy - q, n_y)
            got = slots.at[:, :, yfrom * 2 + core, :, cols(j)]
            remote(got, got, ys_sem.at[q - 1, j], yr_sem.at[yfrom, j], {"dp": partner}).wait_recv()
            fwd.append(remote(got, got, ps_sem.at[q, j], pr_sem.at[yfrom, j], {"dp": partner}))
            fwd[-1].start()
        if j >= 2:
            merge(j - 2)
        for q in range(n_y):
            yfrom = mod(yy - q, n_y)
            got = slots.at[:, :, yfrom * 2 + 1 - core, :, cols(j)]
            remote(got, got, ps_sem.at[q, j], pr_sem.at[yfrom, j], {"dp": partner}).wait_recv()
        main(j)

    total = jnp.sum(gg_acc[...], axis=1, keepdims=True)
    msg_send[:, :cap, :] = jnp.broadcast_to(total, (per, 128)).reshape(n_src, cap, 128)
    square = jnp.sum(jnp.sum(sq_acc[...], axis=1, keepdims=True), axis=0, keepdims=True)
    msg_send[:, cap:, :] = jnp.broadcast_to(square.reshape(1, 1, 1), (n_src, 8, 128))
    m_sends = []
    for k in range(1, n_src):
        to = mod(me + k, n_src)
        m_sends.append(remote(
            msg_send.at[to], msg_recv.at[me], ms_sem.at[k - 1], mr_sem.at[me],
            {"expert": to // n_dp, "dp": lax.rem(to, n_dp)},
        ))
        m_sends[-1].start()
    msg_recv[pl.ds(me, 1)] = msg_send[pl.ds(me, 1)]
    if nj >= 2:
        merge(nj - 2)
    for k in range(1, n_src):
        src = mod(me + k, n_src)
        remote(
            msg_recv.at[src], msg_recv.at[src], ms_sem.at[k - 1], mr_sem.at[src],
            {"expert": src // n_dp, "dp": lax.rem(src, n_dp)},
        ).wait_recv()
    dots = msg_recv[:, :cap, :].reshape(per, 128)
    gg_ref[0:1, :] = jnp.sum(jnp.where(srow == place0, dots, 0.0), axis=0, keepdims=True) / gate0
    gg_ref[1:2, :] = jnp.sum(jnp.where(srow == place1, dots, 0.0), axis=0, keepdims=True) / gate1
    squares = jnp.sum(msg_recv[:, cap:, :], axis=0)
    rms_ref[...] = jnp.sqrt(squares / (n_exp * full * width))
    merge(nj - 1)

    for c in hid_sends + z_sends + fwd + x_sends + m_sends:
        c.wait_send()
    for c in outs:
        c.wait()


def shards(
    cotangent, expert_ids, gate_values, hidden_saved, output_saved,
    weights, moment_one, moment_two, anchor, outer_moment,
):
    n_exp = lax.axis_size("expert")
    n_dp = lax.axis_size("dp")
    n_rep = lax.axis_size("replica")
    toks, width = cotangent.shape[3:]
    full = hidden_saved.shape[6]
    rows = full // n_dp
    ids = expert_ids.reshape(toks, 2).T
    gates = gate_values.reshape(toks, 2).T
    hidden = hidden_saved.reshape(hidden_saved.shape[3:])
    stored = output_saved.reshape(output_saved.shape[3:])
    cap = -(-hidden.shape[2] // 8) * 8
    if cap != hidden.shape[2]:
        more = ((0, 0), (0, 0), (0, cap - hidden.shape[2]), (0, 0))
        hidden, stored = jnp.pad(hidden, more), jnp.pad(stored, more)
    nj = 4
    dc = width // nj
    rblk = 256 if rows % 256 == 0 else 128
    n_src = n_exp * n_dp
    n_y = n_dp // 2
    dims = (n_exp, n_dp, n_rep, cap, rows, width, full, nj, rblk)
    anyspace = pl.BlockSpec(memory_space=pl.ANY)
    vmem = pl.BlockSpec(memory_space=pltpu.VMEM)
    dma = pltpu.SemaphoreType.DMA
    per = n_src * cap
    updated, gg, rms = pl.pallas_call(
        functools.partial(kernel, dims),
        out_shape=(
            jax.ShapeDtypeStruct((rows, width), BF),
            jax.ShapeDtypeStruct((2, toks), F32),
            jax.ShapeDtypeStruct((8, 128), F32),
        ),
        in_specs=[vmem, vmem] + [anyspace] * 8,
        out_specs=(anyspace, vmem, vmem),
        scratch_shapes=[
            pltpu.VMEM((n_dp, n_exp, n_dp, cap, rows), BF),
            pltpu.VMEM((rows, n_dp * per), BF),
            pltpu.VMEM((n_dp, n_exp, n_dp, cap, width), BF),
            pltpu.VMEM((n_exp, n_dp, cap, width), BF),
            pltpu.VMEM((rows, width), BF),
            pltpu.VMEM((rows, width), BF),
            pltpu.VMEM((rows, width), BF),
            pltpu.VMEM((rows // 4, width), F32),
            pltpu.VMEM((rows // 4, width), F32),
            pltpu.VMEM((n_exp, n_dp, cap, width), BF),
            pltpu.VMEM((toks, width), BF),
            pltpu.VMEM((rows // 4, width), BF),
            pltpu.VMEM((rows // 4, width), BF),
            pltpu.VMEM((dc // 128, rblk, 128), F32),
            pltpu.VMEM((per, 128), F32),
            pltpu.VMEM((8, dc), F32),
            pltpu.VMEM((n_src, cap + 8, 128), F32),
            pltpu.VMEM((n_src, cap + 8, 128), F32),
            dma((8,)), dma((nj,)), dma((n_dp,)), dma((n_dp,)),
            dma((n_exp, nj)), dma((n_exp, nj)), dma((n_y, nj)), dma((n_y, nj)),
            dma((n_y, nj)), dma((n_y, nj)), dma((nj,)), dma((nj,)),
            dma((n_src,)), dma((n_src,)),
        ],
        compiler_params=pltpu.CompilerParams(
            collective_id=0, has_side_effects=True, vmem_limit_bytes=62 * 1024 * 1024
        ),
        name="step",
    )(
        ids, gates, cotangent.reshape(toks, width), hidden, stored,
        weights.reshape(rows, width), moment_one.reshape(rows, width), moment_two.reshape(rows, width),
        anchor.reshape(rows // 4, width), outer_moment.reshape(rows // 4, width),
    )
    return (
        updated.reshape(1, 1, rows, width),
        gg.T.reshape(1, 1, 1, toks, 2),
        rms[0, :1],
    )


def solution(mesh):
    return jax.shard_map(
        shards,
        mesh=mesh,
        in_specs=(
            P("replica", "expert", "dp", None, None),
            P("replica", "expert", "dp", None, None),
            P("replica", "expert", "dp", None, None),
            P("replica", "expert", "dp", None, None, None, None),
            P("replica", "expert", "dp", None, None, None, None),
            P("replica", "expert", "dp", None),
            P("replica", "expert", "dp", None),
            P("replica", "expert", "dp", None),
            P("expert", "dp", None),
            P("expert", "dp", None),
        ),
        out_specs=(
            P("replica", "expert", "dp", None),
            P("replica", "expert", "dp", None, None),
            P("replica"),
        ),
        check_vma=False,
    )
```

```python
import functools

import jax
import jax.numpy as jnp
from jax import lax
from jax.experimental import pallas as pl
from jax.experimental.pallas import tpu as pltpu
from jax.sharding import PartitionSpec as P

beta_one = 0.9
beta_two = 0.95
epsilon = 1e-08
inner_rate = 0.3
weight_decay = 0.1
outer_rate = 0.7
nesterov_coef = 0.9

MESH = pl.DeviceIdType.MESH
BF = jnp.bfloat16
F32 = jnp.float32


def kernel(
    dims,
    ids_ref, gates_ref, cot_ref, hid_ref, osv_ref, w_ref, m1_ref, m2_ref, anc_ref, om_ref,
    out_ref, gg_ref, rms_ref,
    hid, hidt, slots, sends, wbuf, m1buf, m2buf, ancbuf, ombuf, osv, cot,
    ids_all, gates_all, frag_send, frag_recv, tmp, gg_acc, sq_acc, msg_send, msg_recv,
    load_sem, out_sem, hs_sem, hr_sem, zs_sem, zr_sem, ys_sem, yr_sem, ps_sem, pr_sem,
    xs_sem, xr_sem, ms_sem, mr_sem,
):
    n_exp, n_dp, n_rep, cap, rows, width, full, nj, rblk = dims
    dc = width // nj
    n_src = n_exp * n_dp
    per = n_src * cap
    depth = n_dp * per
    n_y = n_dp // 2
    e = lax.axis_index("expert")
    d = lax.axis_index("dp")
    r = lax.axis_index("replica")
    me = e * n_dp + d
    core = lax.rem(d, 2)
    yy = d // 2
    partner = yy * 2 + 1 - core
    other = lax.rem(r + 1, n_rep)

    def cols(j):
        return pl.ds(j * dc, dc)

    def remote(src, dst, ssem, rsem, to):
        return pltpu.make_async_remote_copy(
            src_ref=src, dst_ref=dst, send_sem=ssem, recv_sem=rsem,
            device_id=to, device_id_type=MESH,
        )

    def mod(x, n):
        return lax.rem(x + 2 * n, n)

    loads = []
    for i, (src, dst) in enumerate([
        (cot_ref, cot.at[0]), (osv_ref, osv), (w_ref, wbuf), (m1_ref, m1buf),
        (m2_ref, m2buf), (anc_ref, ancbuf), (om_ref, ombuf),
    ]):
        loads.append(pltpu.make_async_copy(src, dst, load_sem.at[i]))
    loads[0].start()

    split = (rows // rblk + 1) // 2 * rblk
    halves = ((0, split), (split, rows - split))

    def hid_cols(to, half):
        start, size = halves[half]
        return pl.ds(pl.multiple_of(to * rows + start, 128), size)

    def own_rows(half):
        start, size = halves[half]
        return pl.ds(start, size)

    hid_own = [
        pltpu.make_async_copy(
            hid_ref.at[:, :, :, hid_cols(d, half)], hid.at[d, :, :, :, own_rows(half)], load_sem.at[7 + half]
        )
        for half in range(2)
    ]

    barrier = pltpu.get_barrier_semaphore()
    for k in range(1, n_src):
        to = mod(me + k, n_src)
        pl.semaphore_signal(barrier, inc=1, device_id={"expert": to // n_dp, "dp": lax.rem(to, n_dp)}, device_id_type=MESH)
    pl.semaphore_signal(barrier, inc=1, device_id={"replica": other}, device_id_type=MESH)
    pl.semaphore_wait(barrier, n_src)

    y_sends = []
    for q in range(1, n_y):
        to = mod(yy + q, n_y) * 2 + core
        for i, (src, dst) in enumerate([(ids_ref, ids_all), (gates_ref, gates_all), (cot_ref, cot)]):
            y_sends.append(remote(src, dst.at[q], ys_sem.at[i, q], yr_sem.at[i, q], {"dp": to}))
            y_sends[-1].start()

    def peer(k, sign):
        if k == n_dp:
            return partner
        return mod(yy + sign * ((k - 2) // 2 + 1), n_y) * 2 + lax.rem(k, 2)

    hid_sends = []
    for half in range(2):
        for k in range(2, n_dp + 1):
            to = peer(k, 1)
            hid_sends.append(remote(
                hid_ref.at[:, :, :, hid_cols(to, half)], hid.at[d, :, :, :, own_rows(half)],
                hs_sem.at[half, k - 2], hr_sem.at[half, d], {"dp": to},
            ))
            hid_sends[-1].start()
        hid_own[half].start()
    for c in loads[1:]:
        c.start()

    toks = ids_ref.shape[1]
    erow = lax.broadcasted_iota(jnp.int32, (8 * ((n_exp + 7) // 8), toks), 0)
    earlier = (
        lax.broadcasted_iota(jnp.int32, (toks, toks), 0) < lax.broadcasted_iota(jnp.int32, (toks, toks), 1)
    ).astype(F32).astype(BF)
    srow = lax.broadcasted_iota(jnp.int32, (per, toks), 0)
    shift = n_dp.bit_length() - 1

    def places(both):
        counts = ((both[0:1] == erow).astype(F32) + (both[1:2] == erow).astype(F32)).astype(BF)
        ranks = jnp.dot(counts, earlier, preferred_element_type=F32)

        def place(ids):
            rank = jnp.sum(jnp.where(ids == erow, ranks, 0.0), axis=0, keepdims=True).astype(jnp.int32)
            return (ids * n_dp + (rank & (n_dp - 1))) * cap + (rank >> shift)

        return place(both[0:1]), place(both[1:2])

    def table(both, gates):
        place0, place1 = places(both)
        gate_slot = jnp.sum(
            jnp.where(srow == place0, gates[0:1], 0.0) + jnp.where(srow == place1, gates[1:2], 0.0),
            axis=1, keepdims=True,
        )
        return ((srow == place0).astype(F32) + (srow == place1).astype(F32)).astype(BF), gate_slot

    z_sends = []

    def fill(q, j, onehot, gate_slot):
        lo, hi = j * dc, (j + 1) * dc
        row = mod(yy - q, n_y)
        rows_j = jnp.dot(onehot, cot[q, :, lo:hi], preferred_element_type=F32)
        sends[q, :, :, :, lo:hi] = (gate_slot * rows_j).astype(BF).reshape(n_exp, n_dp, cap, dc)
        for k in range(1, n_exp):
            to = mod(e + k, n_exp)
            z_sends.append(remote(
                sends.at[q, to, :, :, cols(j)], slots.at[:, e, row, core, :, cols(j)],
                zs_sem.at[q, k - 1, j], zr_sem.at[q, e, j], {"expert": to},
            ))
            z_sends[-1].start()
        slots[:, pl.ds(e, 1), pl.ds(row, 1), pl.ds(core, 1), :, lo:hi] = (
            sends[q, pl.ds(e, 1), :, :, lo:hi].reshape(n_dp, 1, 1, 1, cap, dc)
        )

    loads[0].wait()
    tables = [table(ids_ref[...], gates_ref[...])]
    fill(0, 0, *tables[0])
    if nj > 1:
        fill(0, 1, *tables[0])
    for q in range(1, n_y):
        h = mod(yy - q, n_y) * 2 + core
        for i, (src, dst) in enumerate([(ids_ref, ids_all), (gates_ref, gates_all), (cot_ref, cot)]):
            remote(src, dst.at[q], ys_sem.at[i, q], yr_sem.at[i, q], {"dp": h}).wait_recv()
        tables.append(table(ids_all[q], gates_all[q]))
    for j in range(nj):
        for q in range(n_y):
            if q > 0 or j > 1:
                fill(q, j, *tables[q])

    fwd = []

    def column(j):
        for k in range(1, n_exp):
            a = mod(e + k, n_exp)
            for q in range(n_y):
                remote(
                    sends.at[q, a, :, :, cols(j)], slots.at[:, a, mod(yy - q, n_y), core, :, cols(j)],
                    zs_sem.at[q, k - 1, j], zr_sem.at[q, a, j], {"expert": a},
                ).wait_recv()
        mine = slots.at[:, :, :, core, :, cols(j)]
        fwd.append(remote(mine, mine, ps_sem.at[j], pr_sem.at[j], {"dp": partner}))
        fwd[-1].start()

    def partner_column(j):
        got = slots.at[:, :, :, 1 - core, :, cols(j)]
        remote(got, got, ps_sem.at[j], pr_sem.at[j], {"dp": partner}).wait_recv()

    def turn(h, half):
        start, size = halves[half]
        for s in range(start, start + size, 128):
            block = hid[pl.ds(h, 1), :, :, :, s:s + 128].reshape(per, 128)
            hidt[s:s + 128, pl.ds(pl.multiple_of(h * per, 128), per)] = block.T

    def near(half):
        hid_own[half].wait()
        turn(d, half)

    def far(half):
        for k in range(n_dp, 1, -1):
            h = peer(k, -1)
            dst = hid.at[h, :, :, :, own_rows(half)]
            remote(dst, dst, hs_sem.at[half, k - 2], hr_sem.at[half, h], {"dp": h}).wait_recv()
            turn(h, half)

    sq_acc[...] = jnp.zeros_like(sq_acc)
    gg_acc[...] = jnp.zeros_like(gg_acc)
    x_sends, outs = {}, []
    fblk = rblk // 4

    def products(j):
        lo, hi = j * dc, (j + 1) * dc
        prod = (
            slots[pl.ds(d, 1), :, :, :, :, lo:hi].reshape(per, dc).astype(F32)
            * osv[:, :, :, lo:hi].reshape(per, dc).astype(F32)
        )
        part = prod[:, :128]
        for s in range(128, dc, 128):
            part = part + prod[:, s:s + 128]
        gg_acc[...] += part

    def main(half, j):
        lo, hi = j * dc, (j + 1) * dc
        start, size = halves[half]
        right = slots[:, :, :, :, :, lo:hi].reshape(depth, dc)

        def step(i, _):
            here = pl.ds(pl.multiple_of(i * rblk, rblk), rblk)
            g = jnp.dot(hidt[here, :], right, preferred_element_type=F32)
            sq_acc[...] += jnp.sum((g * g).reshape(rblk // 8, 8, dc), axis=0)
            first = beta_one * m1buf[here, lo:hi].astype(F32) + (1.0 - beta_one) * g
            second = beta_two * m2buf[here, lo:hi].astype(F32) + (1.0 - beta_two) * g * g
            old = wbuf[here, lo:hi].astype(F32)
            new = old - inner_rate * (first / (jnp.sqrt(second) + epsilon) + weight_decay * old)
            wbuf[here, lo:hi] = new.astype(BF)
            for s in range(0, dc, 128):
                tmp[s // 128] = new[:, s:s + 128]
                frag_send[pl.ds(pl.multiple_of(i * fblk, fblk), fblk), lo + s:lo + s + 128] = (
                    tmp[s // 128, pl.ds(0, fblk, stride=4), :].astype(BF)
                )
            return 0

        lax.fori_loop(start // rblk, (start + size) // rblk, step, 0)
        part = frag_part(half)
        x_sends[half, j] = remote(
            frag_send.at[part, cols(j)], frag_recv.at[part, cols(j)],
            xs_sem.at[half, j], xr_sem.at[half, j], {"replica": other},
        )
        x_sends[half, j].start()

    def frag_part(half):
        start, size = halves[half]
        return pl.ds(start // 4, size // 4)

    def merge(half, j):
        lo, hi = j * dc, (j + 1) * dc
        start_row, size = halves[half]
        x_sends[half, j].wait_recv()

        def step(i, _):
            here = pl.ds(pl.multiple_of(i * rblk, rblk), rblk)
            there = pl.ds(pl.multiple_of(i * fblk, fblk), fblk)
            start = ancbuf[there, lo:hi]
            summed = (start - frag_send[there, lo:hi].astype(F32)) + (start - frag_recv[there, lo:hi].astype(F32))
            average = summed / n_rep
            momentum = nesterov_coef * ombuf[there, lo:hi] + average
            point = start - outer_rate * (average + nesterov_coef * momentum)
            for s in range(0, dc, 128):
                tmp[s // 128] = wbuf[here, lo + s:lo + s + 128].astype(F32)
                tmp[s // 128, pl.ds(0, fblk, stride=4), :] = point[:, s:s + 128]
                wbuf[here, lo + s:lo + s + 128] = tmp[s // 128].astype(BF)
            return 0

        lax.fori_loop(start_row // rblk, (start_row + size) // rblk, step, 0)
        whole = own_rows(half)
        outs.append(pltpu.make_async_copy(
            wbuf.at[whole, cols(j)], out_ref.at[whole, cols(j)], out_sem.at[half, j]
        ))
        outs[-1].start()

    near(0)
    column(0)
    far(0)
    for c in loads[1:]:
        c.wait()
    last = nj - 1
    order = []
    for j in range(last):
        if j > 0:
            column(j)
        partner_column(j)
        products(j)
        main(0, j)
        order.append((0, j))
        if j == 0:
            near(1)
        if j > 0:
            merge(*order[j - 1])
    merged = last - 1
    far(1)
    column(last)
    for j in range(last):
        main(1, j)
        order.append((1, j))
        merge(*order[merged])
        merged += 1
    partner_column(last)
    products(last)
    for half in range(2):
        main(half, last)
        order.append((half, last))
        if half == 0:
            merge(*order[merged])
            merged += 1

    total = jnp.sum(gg_acc[...], axis=1, keepdims=True)
    msg_send[:, :cap, :] = jnp.broadcast_to(total, (per, 128)).reshape(n_src, cap, 128)
    square = jnp.sum(jnp.sum(sq_acc[...], axis=1, keepdims=True), axis=0, keepdims=True)
    msg_send[:, cap:, :] = jnp.broadcast_to(square.reshape(1, 1, 1), (n_src, 8, 128))
    m_sends = []
    for k in range(1, n_src):
        to = mod(me + k, n_src)
        m_sends.append(remote(
            msg_send.at[to], msg_recv.at[me], ms_sem.at[k - 1], mr_sem.at[me],
            {"expert": to // n_dp, "dp": lax.rem(to, n_dp)},
        ))
        m_sends[-1].start()
    msg_recv[pl.ds(me, 1)] = msg_send[pl.ds(me, 1)]
    while merged < len(order) - 1:
        merge(*order[merged])
        merged += 1
    for k in range(1, n_src):
        src = mod(me + k, n_src)
        remote(
            msg_recv.at[src], msg_recv.at[src], ms_sem.at[k - 1], mr_sem.at[src],
            {"expert": src // n_dp, "dp": lax.rem(src, n_dp)},
        ).wait_recv()
    place0, place1 = places(ids_ref[...])
    gate0, gate1 = gates_ref[0:1, :], gates_ref[1:2, :]
    dots = msg_recv[:, :cap, :].reshape(per, 128)
    gg_ref[0:1, :] = jnp.sum(jnp.where(srow == place0, dots, 0.0), axis=0, keepdims=True) / gate0
    gg_ref[1:2, :] = jnp.sum(jnp.where(srow == place1, dots, 0.0), axis=0, keepdims=True) / gate1
    squares = jnp.sum(msg_recv[:, cap:, :], axis=0)
    rms_ref[...] = jnp.sqrt(squares / (n_exp * full * width))
    merge(*order[merged])

    for c in y_sends + hid_sends + z_sends + fwd + list(x_sends.values()) + m_sends:
        c.wait_send()
    for c in outs:
        c.wait()


def shards(
    cotangent, expert_ids, gate_values, hidden_saved, output_saved,
    weights, moment_one, moment_two, anchor, outer_moment,
):
    n_exp = lax.axis_size("expert")
    n_dp = lax.axis_size("dp")
    n_rep = lax.axis_size("replica")
    toks, width = cotangent.shape[3:]
    full = hidden_saved.shape[6]
    rows = full // n_dp
    ids = expert_ids.reshape(toks, 2).T
    gates = gate_values.reshape(toks, 2).T
    hidden = hidden_saved.reshape(hidden_saved.shape[3:])
    stored = output_saved.reshape(output_saved.shape[3:])
    cap = -(-hidden.shape[2] // 8) * 8
    if cap != hidden.shape[2]:
        more = ((0, 0), (0, 0), (0, cap - hidden.shape[2]), (0, 0))
        hidden, stored = jnp.pad(hidden, more), jnp.pad(stored, more)
    nj = 4
    dc = width // nj
    rblk = 256 if rows % 256 == 0 else 128
    n_src = n_exp * n_dp
    n_y = n_dp // 2
    dims = (n_exp, n_dp, n_rep, cap, rows, width, full, nj, rblk)
    anyspace = pl.BlockSpec(memory_space=pl.ANY)
    vmem = pl.BlockSpec(memory_space=pltpu.VMEM)
    dma = pltpu.SemaphoreType.DMA
    per = n_src * cap
    updated, gg, rms = pl.pallas_call(
        functools.partial(kernel, dims),
        out_shape=(
            jax.ShapeDtypeStruct((rows, width), BF),
            jax.ShapeDtypeStruct((2, toks), F32),
            jax.ShapeDtypeStruct((8, 128), F32),
        ),
        in_specs=[vmem, vmem] + [anyspace] * 8,
        out_specs=(anyspace, vmem, vmem),
        scratch_shapes=[
            pltpu.VMEM((n_dp, n_exp, n_dp, cap, rows), BF),
            pltpu.VMEM((rows, n_dp * per), BF),
            pltpu.VMEM((n_dp, n_exp, n_y, 2, cap, width), BF),
            pltpu.VMEM((n_y, n_exp, n_dp, cap, width), BF),
            pltpu.VMEM((rows, width), BF),
            pltpu.VMEM((rows, width), BF),
            pltpu.VMEM((rows, width), BF),
            pltpu.VMEM((rows // 4, width), F32),
            pltpu.VMEM((rows // 4, width), F32),
            pltpu.VMEM((n_exp, n_dp, cap, width), BF),
            pltpu.VMEM((n_y, toks, width), BF),
            pltpu.VMEM((n_y, 2, toks), jnp.int32),
            pltpu.VMEM((n_y, 2, toks), F32),
            pltpu.VMEM((rows // 4, width), BF),
            pltpu.VMEM((rows // 4, width), BF),
            pltpu.VMEM((dc // 128, rblk, 128), F32),
            pltpu.VMEM((per, 128), F32),
            pltpu.VMEM((8, dc), F32),
            pltpu.VMEM((n_src, cap + 8, 128), F32),
            pltpu.VMEM((n_src, cap + 8, 128), F32),
            dma((9,)), dma((2, nj)), dma((2, n_dp)), dma((2, n_dp)),
            dma((n_y, n_exp, nj)), dma((n_y, n_exp, nj)), dma((3, n_y)), dma((3, n_y)),
            dma((nj,)), dma((nj,)), dma((2, nj)), dma((2, nj)),
            dma((n_src,)), dma((n_src,)),
        ],
        compiler_params=pltpu.CompilerParams(
            collective_id=0, has_side_effects=True, vmem_limit_bytes=62 * 1024 * 1024
        ),
        name="step",
    )(
        ids, gates, cotangent.reshape(toks, width), hidden, stored,
        weights.reshape(rows, width), moment_one.reshape(rows, width), moment_two.reshape(rows, width),
        anchor.reshape(rows // 4, width), outer_moment.reshape(rows // 4, width),
    )
    return (
        updated.reshape(1, 1, rows, width),
        gg.T.reshape(1, 1, 1, toks, 2),
        rms[0, :1],
    )


def solution(mesh):
    return jax.shard_map(
        shards,
        mesh=mesh,
        in_specs=(
            P("replica", "expert", "dp", None, None),
            P("replica", "expert", "dp", None, None),
            P("replica", "expert", "dp", None, None),
            P("replica", "expert", "dp", None, None, None, None),
            P("replica", "expert", "dp", None, None, None, None),
            P("replica", "expert", "dp", None),
            P("replica", "expert", "dp", None),
            P("replica", "expert", "dp", None),
            P("expert", "dp", None),
            P("expert", "dp", None),
        ),
        out_specs=(
            P("replica", "expert", "dp", None),
            P("replica", "expert", "dp", None, None),
            P("replica"),
        ),
        check_vma=False,
    )
```
